256 devices in a mesh: seq: 32 (over x, z), head: 8 (over y, core).
Axes of the slice: x: 4, y: 4, z: 8, core: 2. Of those that a mesh axis runs over, the one named last changes fastest.
Arguments:
- layer_input: bfloat16 [8192, 4096], P('seq', 'head'), may hold values from -6 to 6
- value_weight: bfloat16 [4096, 4096], P(None, 'head'), may hold values from -0.09375 to 0.09375
- state_weight: bfloat16 [4096, 2048], P(None, 'head'), may hold values from -0.02734375 to 0.02734375
- output_weight: bfloat16 [4096, 4096], P('head'), may hold values from -0.09375 to 0.09375
- log_decay: float32 [64, 8192], P('head', 'seq'), may hold values from -1.5 to 0, as said below
- skip_gain: float32 [64], P('head'), may hold values from 0.5 to 1.5
- output_grad: bfloat16 [8192, 4096], P('seq', 'head'), may hold values from -6 to 6
Outputs:
- layer_output: bfloat16 [8192, 4096], P('seq', 'head')
- input_grad: bfloat16 [8192, 4096], P('seq', 'head')
The draws below stay inside these ranges and needn't reach their ends.
Inputs may be any that keep to these rules, and one draw needn't show every extreme that they name: `log_decay`: each entry is below zero.
All inputs are finite; a program needn't handle non-finite values.
Results may differ from the reference program's by a relative error of at most 0.015.
Values may be sent and summed in bfloat16 or wider, within the bound.
No kernel may reach another device: no remote copies, remote signals or barrier semaphores. Data moves between devices by JAX's collectives and lax.ppermute only.
A program may use at most 64 MiB of HBM per device.

```python
import jax
import jax.numpy as jnp
from jax import lax

D = 4096
MIXER_HEADS = 64
HEAD_DIM = 64
STATE = 128
GROUPS = 8
BLOCK = 256
TOK_DEV = 256
SEQUENCE_TOKENS = 8192
INNER = 4096


def draw_log_decay(key, part):
    random_subkeys = jax.random.split(key, 7)
    fast_share = 0.4
    fast_heads = jax.random.bernoulli(random_subkeys[0], fast_share, (MIXER_HEADS, 1))
    fast_rate = jnp.exp(jax.random.uniform(random_subkeys[1], (MIXER_HEADS, 1), jnp.float32, jnp.log(1.0 / 50.0), jnp.log(1.0 / 30.0)))
    slow_rate = jnp.exp(jax.random.uniform(random_subkeys[2], (MIXER_HEADS, 1), jnp.float32, jnp.log(0.1), jnp.log(0.5))) / SEQUENCE_TOKENS
    blocks = SEQUENCE_TOKENS // TOK_DEV
    factor = jnp.exp(jax.random.uniform(random_subkeys[3], (MIXER_HEADS, blocks, 1), jnp.float32, jnp.log(0.5), jnp.log(1.5)))
    factor = jnp.broadcast_to(factor, (MIXER_HEADS, blocks, TOK_DEV)).reshape(MIXER_HEADS, SEQUENCE_TOKENS)
    roughness = jax.random.uniform(random_subkeys[4], (MIXER_HEADS, SEQUENCE_TOKENS), jnp.float32, 0.5, 1.5)
    decay_speed = jnp.where(fast_heads, fast_rate, slow_rate) * factor * roughness
    positions_list = jax.random.randint(random_subkeys[5], (MIXER_HEADS, 2, 1), 0, SEQUENCE_TOKENS)
    surge_depth = jax.random.uniform(random_subkeys[6], (MIXER_HEADS, 2, 1), jnp.float32, jnp.log(0.5), jnp.log(0.8))
    surge_hits = jnp.arange(SEQUENCE_TOKENS, dtype=jnp.int32)[None, None, :] == positions_list
    surge_total = jnp.sum(jnp.where(surge_hits, surge_depth, 0.0), axis=1)
    return (surge_total - decay_speed).astype(jnp.float32)


def level_of(rng, extent, cuts, least, high):
    factor_of = 1.0
    for dim, shards_of in cuts:
        heights = jax.random.uniform(jax.random.fold_in(jax.random.fold_in(rng, 6), dim), (shards_of,), jnp.float32, least / len(cuts), high / len(cuts))
        factor_of = factor_of * jnp.repeat(jnp.exp(heights), extent[dim] // shards_of).reshape((-1,) + (1,) * (len(extent) - 1 - dim))
    return factor_of


def bell_draw(stream_key, dims, scale, most, cuts=(), kind=jnp.bfloat16):
    drawn = jax.random.normal(stream_key, dims, jnp.float32) * scale
    if len(cuts) > 0:
        drawn = level_of(stream_key, dims, cuts, -0.22, 0.18) * drawn
    return jnp.clip(drawn, min=-most, max=most).astype(kind)


def setup_inputs(seed: int = 0) -> dict:
    splits = jax.random.split(jax.random.key(seed), 8)
    return {
        "layer_input": bell_draw(splits[0], (SEQUENCE_TOKENS, D), 1.0, 6.0, ((0, 32), (1, 8))),
        "value_weight": bell_draw(splits[1], (D, INNER), D ** -0.5, 0.09375, ((1, 8),)),
        "state_weight": bell_draw(splits[2], (D, 2 * STATE * GROUPS), (11 * D) ** -0.5, 0.02734375, ((1, 8),)),
        "output_weight": bell_draw(splits[3], (INNER, D), INNER ** -0.5, 0.09375, ((0, 8),)),
        "log_decay": draw_log_decay(jax.random.fold_in(splits[7], 71), 0),
        "skip_gain": jnp.clip(0.5 + 1.0 * jax.random.uniform(splits[5], (MIXER_HEADS,), jnp.float32) ** level_of(splits[5], (MIXER_HEADS,), ((0, 8),), -0.2, 0.2), 0.5, 1.5),
        "output_grad": bell_draw(splits[6], (SEQUENCE_TOKENS, D), 1.0, 6.0, ((0, 32), (1, 8))),
    }


highest = lax.Precision.HIGHEST

def block_step(carried, pieces):
    values, writer, reader, decays = pieces
    running = jnp.cumsum(decays, axis=-1)
    inflow = jnp.sqrt(-jnp.expm1(2.0 * decays))
    length = decays.shape[-1]
    causal = jnp.arange(length)[:, None] >= jnp.arange(length)[None, :]
    spread = running[..., :, None] - running[..., None, :]
    kernel = jnp.where(causal, jnp.exp(jnp.where(causal, spread, 0.0)), 0.0)
    scores = jnp.einsum('tgn,sgn->gts', reader, writer, precision=highest)
    weights = scores[:, None] * kernel * inflow[..., None, :]
    within = jnp.einsum('ghts,sghp->tghp', weights, values, precision=highest)
    entering = jnp.transpose(jnp.exp(running), (2, 0, 1))[..., None]
    carried_part = jnp.einsum('tgn,ghnp->tghp', reader, carried, precision=highest) * entering
    to_end = jnp.exp(running[..., -1:] - running) * inflow
    fresh_part = jnp.einsum('sgn,ghs,sghp->ghnp', writer, to_end, values, precision=highest)
    carried = jnp.exp(running[..., -1])[..., None, None] * carried + fresh_part
    return (carried, within + carried_part)

def scan_blocks(values, writer, reader, decays, carried, block_rows, step_function):
    total_rows, group_count, per_group, head_width = values.shape
    block_count = total_rows // block_rows
    pieces = (values.reshape(block_count, block_rows, group_count, per_group, head_width), writer.reshape(block_count, block_rows, group_count, writer.shape[-1]), reader.reshape(block_count, block_rows, group_count, reader.shape[-1]), jnp.moveaxis(decays.reshape(group_count, per_group, block_count, block_rows), 2, 0))
    carried, outputs = lax.scan(step_function, carried, pieces)
    return (carried, outputs.reshape(total_rows, group_count, per_group, head_width))

def mixer_pass(value_input, pair_input, log_decay, skip_gain):
    total_rows = value_input.shape[0]
    per_group = MIXER_HEADS // GROUPS
    head_values = value_input.reshape(total_rows, GROUPS, per_group, HEAD_DIM)
    pair_split = pair_input.reshape(total_rows, GROUPS, 2, STATE)
    decays = log_decay.reshape(GROUPS, per_group, total_rows)
    zero_state = jnp.zeros((GROUPS, per_group, STATE, HEAD_DIM), jnp.float32)
    final_state, outputs = scan_blocks(head_values, pair_split[:, :, 0], pair_split[:, :, 1], decays, zero_state, BLOCK, jax.checkpoint(block_step))
    outputs = outputs + skip_gain.reshape(GROUPS, per_group)[None, :, :, None] * head_values
    return outputs.reshape(total_rows, MIXER_HEADS * HEAD_DIM)

def reference(layer_input, value_weight, state_weight, output_weight, log_decay, skip_gain, output_grad):
    values = jnp.dot(layer_input, value_weight, preferred_element_type=jnp.float32).astype(jnp.bfloat16)
    pair_rows = jnp.dot(layer_input, state_weight, preferred_element_type=jnp.float32).astype(jnp.bfloat16)
    values = lax.optimization_barrier(values)
    pair_rows = lax.optimization_barrier(pair_rows)

    def through(value_input, pair_input):
        return mixer_pass(value_input, pair_input, log_decay, skip_gain)
    mixed_full, pullback = jax.vjp(through, values.astype(jnp.float32), pair_rows.astype(jnp.float32))
    mixer_out = mixed_full.astype(jnp.bfloat16)
    layer_output = jnp.dot(mixer_out, output_weight, preferred_element_type=jnp.float32).astype(jnp.bfloat16)
    mixed_grad = jnp.dot(output_grad, output_weight.T, preferred_element_type=jnp.float32).astype(jnp.bfloat16)
    value_grad, pair_grad = pullback(mixed_grad.astype(jnp.float32))
    input_grad = jnp.dot(value_grad.astype(jnp.bfloat16), value_weight.T, preferred_element_type=jnp.float32)
    input_grad = input_grad + jnp.dot(pair_grad.astype(jnp.bfloat16), state_weight.T, preferred_element_type=jnp.float32)
    return (layer_output, input_grad.astype(jnp.bfloat16))
```

```python
import functools

import jax
import jax.numpy as jnp
from jax import lax
from jax.experimental import pallas as pl
from jax.experimental.pallas import tpu as pltpu
from jax.sharding import Mesh
from jax.sharding import PartitionSpec as P


STATE = 128
SEQ = ("x", "z")
F32 = jnp.float32
BF16 = jnp.bfloat16
NN = (((1,), (0,)), ((), ()))
NT = (((1,), (1,)), ((), ()))
TN = (((0,), (0,)), ((), ()))


def dot(a, b, dims):
    return lax.dot_general(a, b, dims, preferred_element_type=F32)


def call(body, outs, *args, flops=0):
    moved = sum(a.size * a.dtype.itemsize for a in args) + sum(
        o.size * o.dtype.itemsize for o in outs
    )
    return pl.pallas_call(
        body,
        out_shape=outs,
        in_specs=[pl.BlockSpec(memory_space=pltpu.VMEM)] * len(args),
        out_specs=[pl.BlockSpec(memory_space=pltpu.VMEM)] * len(outs),
        cost_estimate=pl.CostEstimate(flops=flops, bytes_accessed=moved, transcendentals=0),
    )(*args)


def shift(array, axis, step):
    size = lax.axis_size(axis)
    return lax.ppermute(array, axis, [(i, (i + step) % size) for i in range(size)])


def end_state_kernel(pair_ref, value_ref, scale_ref, first, state_ref):
    scaled = (value_ref[...].astype(F32) * scale_ref[...]).astype(BF16)
    columns = pair_ref[:, first : first + STATE]
    state_ref[...] = dot(columns, scaled, TN).astype(BF16)


def state_of(pair, value, scale, first):
    def body(pair_ref, value_ref, scale_ref, state_ref):
        end_state_kernel(pair_ref, value_ref, scale_ref, first, state_ref)

    return call(
        body, [jax.ShapeDtypeStruct((STATE, value.shape[1]), BF16)], pair, value, scale, flops=2**25
    )[0]


def prefix_kernel(reverse, pieces_ref, decay_ref, out_ref):
    count = pieces_ref.shape[0]
    state = jnp.zeros(pieces_ref.shape[1:], F32)
    for k in reversed(range(count)) if reverse else range(count):
        out_ref[k] = state.astype(BF16)
        state = state * decay_ref[k : k + 1, :] + pieces_ref[k].astype(F32)


def prefix(pieces, decay, reverse):
    return call(
        functools.partial(prefix_kernel, reverse),
        [jax.ShapeDtypeStruct(pieces.shape, BF16)],
        pieces,
        decay,
    )[0]


def masked(pair, odd):
    lane = lax.broadcasted_iota(jnp.int32, pair.shape, 1)
    keep = lane >= 64 if odd else lane < 64
    return jnp.where(keep, pair, jnp.zeros_like(pair))


def decay_matrix(h, run_row_ref, run_col_ref, inflow_ref):
    rows = run_row_ref.shape[1]
    t = lax.broadcasted_iota(jnp.int32, (rows, rows), 0)
    s = lax.broadcasted_iota(jnp.int32, (rows, rows), 1)
    spread = run_col_ref[:, h : h + 1] - run_row_ref[h : h + 1, :]
    spread = jnp.where(t >= s, spread, -1e30)
    return jnp.exp(spread) * inflow_ref[h : h + 1, :]


def forward_kernel(
    pair_ref, value_ref, run_row_ref, run_col_ref, inflow_ref, skip_ref, local_ref, weight_ref, decay_ref
):
    scores = dot(pair_ref[:, STATE:], pair_ref[:, :STATE], NT)
    for two in range(4):
        columns = slice(two * 128, two * 128 + 128)
        value_pair = value_ref[:, columns]
        total = value_pair.astype(F32) * skip_ref[:, columns]
        for odd in range(2):
            h = 2 * two + odd
            decay = decay_matrix(h, run_row_ref, run_col_ref, inflow_ref)
            weight = (scores * decay).astype(BF16)
            weight_ref[h] = weight
            decay_ref[h] = decay.astype(BF16)
            total = total + dot(weight, masked(value_pair, odd), NN)
        local_ref[:, columns] = total


def backward_kernel(
    pair_ref, value_ref, grad_ref, skip_ref, weight_ref, decay_ref, value_grad_ref, pair_grad_ref
):
    rows = pair_ref.shape[0]
    score_grad = jnp.zeros((rows, rows), F32)
    for two in range(4):
        columns = slice(two * 128, two * 128 + 128)
        value_pair = value_ref[:, columns]
        grad_pair = grad_ref[:, columns]
        total = grad_pair.astype(F32) * skip_ref[:, columns]
        for odd in range(2):
            h = 2 * two + odd
            grad_one = masked(grad_pair, odd)
            weight_grad = dot(grad_one, value_pair, NT)
            score_grad = score_grad + weight_grad * decay_ref[h].astype(F32)
            total = total + dot(weight_ref[h], grad_one, TN)
        value_grad_ref[:, columns] = total
    score_grad = score_grad.astype(BF16)
    pair_grad_ref[:, :STATE] = dot(score_grad, pair_ref[:, STATE:], TN)
    pair_grad_ref[:, STATE:] = dot(score_grad, pair_ref[:, :STATE], NN)


def output_kernel(pair_ref, state_ref, entering_ref, local_ref, out_ref):
    carried = dot(pair_ref[:, STATE:], state_ref[...], NN) * entering_ref[...]
    out_ref[...] = (local_ref[...] + carried).astype(BF16)


def gradient_kernel(
    pair_ref,
    value_ref,
    grad_ref,
    incoming_ref,
    outgoing_ref,
    entering_ref,
    to_end_ref,
    value_grad_ref,
    pair_grad_ref,
    out_ref,
):
    width = value_ref.shape[1]
    outgoing = outgoing_ref[...]
    carried = dot(pair_ref[:, :STATE], outgoing, NN) * to_end_ref[...]
    out_ref[:, :width] = (value_grad_ref[...] + carried).astype(BF16)
    value_scaled = (value_ref[...].astype(F32) * to_end_ref[...]).astype(BF16)
    writer = pair_grad_ref[:, :STATE] + dot(value_scaled, outgoing, NT)
    out_ref[:, width : width + STATE] = writer.astype(BF16)
    grad_scaled = (grad_ref[...].astype(F32) * entering_ref[...]).astype(BF16)
    reader = pair_grad_ref[:, STATE:] + dot(grad_scaled, incoming_ref[...], NT)
    out_ref[:, width + STATE :] = reader.astype(BF16)


def gather(own):
    half = own.shape[0] // 2
    from_low = shift(own, "y", 1)
    from_high = shift(own, "y", -1)
    far_top = shift(from_low[:half], "y", 1)
    far_bottom = shift(from_high[half:], "y", -1)
    far = jnp.concatenate([far_top, far_bottom], axis=0)
    mine = {0: own, 1: from_low, 3: from_high, 2: far}
    pieces = []
    for back in (0, 1, 3, 2):
        pieces.append((back, 0, mine[back]))
        pieces.append((back, 1, shift(mine[back], "c", 1)))
    return pieces


def scatter(block):
    last = block(2).astype(BF16)
    half = last.shape[0] // 2
    from_low = shift(last[:half], "y", 1)
    from_high = shift(last[half:], "y", -1)
    up, down = block(1), block(3)
    up = jnp.concatenate([up[:half] + from_low.astype(F32), up[half:]], axis=0).astype(BF16)
    down = jnp.concatenate([down[:half], down[half:] + from_high.astype(F32)], axis=0).astype(BF16)
    from_low = shift(up, "y", 1)
    from_high = shift(down, "y", -1)
    total = block(0) + from_low.astype(F32) + from_high.astype(F32)
    return total.astype(BF16)


def per_device(
    layer_input, value_weight, state_weight, output_weight, log_decay, skip_gain, output_grad
):
    rows, shard = layer_input.shape
    heads = log_decay.shape[0]
    width = value_weight.shape[1]
    head_width = width // heads
    y, c = lax.axis_index("y"), lax.axis_index("c")

    def start(back, other):
        return (((y - back) % 4) * 2 + jnp.where(other == 1, 1 - c, c)) * shard

    def expand(per_head):
        return jnp.repeat(per_head, head_width, axis=-1)

    def exchange(state):
        pieces = state.reshape(32, -1, width)
        return lax.all_to_all(pieces, SEQ, 0, 0, tiled=True)

    inflow = jnp.sqrt(-jnp.expm1(2.0 * log_decay))
    run = jnp.cumsum(log_decay, axis=-1)
    run_col = run.T
    entering = expand(jnp.exp(run_col))
    to_end = expand((jnp.exp(run[:, -1:] - run) * inflow).T)
    total = expand(run[:, -1])[None]
    skip = expand(skip_gain)[None]
    totals = lax.all_to_all(jnp.broadcast_to(total, (32, width)), SEQ, 0, 0, tiled=True)
    decays = jnp.exp(totals)

    value_sum = jnp.zeros((rows, width), F32)
    pair_sum = jnp.zeros((rows, state_weight.shape[1]), F32)
    for back, other, piece in gather(layer_input):
        at = start(back, other)
        value_sum += dot(piece, lax.dynamic_slice_in_dim(value_weight, at, shard, 0), NN)
        pair_sum += dot(piece, lax.dynamic_slice_in_dim(state_weight, at, shard, 0), NN)
    values = value_sum.astype(BF16)
    pair = pair_sum.astype(BF16)
    arrived = exchange(state_of(pair, values, to_end, 0))
    incoming = exchange(prefix(arrived, decays, False)).reshape(STATE, width)

    grad_sum = jnp.zeros((rows, width), F32)
    for back, other, piece in gather(output_grad):
        at = start(back, other)
        grad_sum += dot(piece, lax.dynamic_slice_in_dim(output_weight, at, shard, 1), NT)
    mixed_grad = grad_sum.astype(BF16)
    arrived_back = exchange(state_of(pair, mixed_grad, entering, STATE))
    outgoing = exchange(prefix(arrived_back, decays, True)).reshape(STATE, width)

    square = jax.ShapeDtypeStruct((heads, rows, rows), BF16)
    wide = jax.ShapeDtypeStruct((rows, width), F32)
    local, weights, kernels = call(
        forward_kernel, [wide, square, square], pair, values, run, run_col, inflow, skip, flops=2**27
    )
    value_grad, pair_grad = call(
        backward_kernel,
        [wide, jax.ShapeDtypeStruct((rows, 2 * STATE), F32)],
        pair,
        values,
        mixed_grad,
        skip,
        weights,
        kernels,
        flops=2**28,
    )

    value_weight, state_weight, output_weight, mixed_grad = lax.optimization_barrier(
        (value_weight, state_weight, output_weight, mixed_grad)
    )
    value_rows = value_weight.reshape(4, 2, shard, width)
    state_rows = state_weight.reshape(4, 2, shard, 2 * STATE)
    out_columns = output_weight.reshape(width, 4, 2, shard)

    def of_core(array, core, axis):
        return lax.dynamic_index_in_dim(array, core, axis, keepdims=False)

    value_other = shift(of_core(value_rows, 1 - c, 1), "c", 1)
    state_other = shift(of_core(state_rows, 1 - c, 1), "c", 1)
    out_other = shift(of_core(out_columns, 1 - c, 2), "c", 1)
    value_own = of_core(value_rows, c, 1)
    state_own = of_core(state_rows, c, 1)
    out_own = of_core(out_columns, c, 2)

    mixer_out = call(
        output_kernel,
        [jax.ShapeDtypeStruct((rows, width), BF16)],
        pair,
        incoming,
        entering,
        local,
        flops=2**25,
    )[0]
    mixer_other = shift(mixer_out, "c", 1)

    def output_block(ahead):
        at = (y + ahead) % 4
        return dot(mixer_out, of_core(out_own, at, 1), NN) + dot(
            mixer_other, of_core(out_other, at, 1), NN
        )

    layer_output = scatter(output_block)

    grads = call(
        gradient_kernel,
        [jax.ShapeDtypeStruct((rows, width + 2 * STATE), BF16)],
        pair,
        values,
        mixed_grad,
        incoming,
        outgoing,
        entering,
        to_end,
        value_grad,
        pair_grad,
        flops=2**27,
    )[0]
    grads_other = shift(grads, "c", 1)

    def input_block(ahead):
        at = (y + ahead) % 4
        return (
            dot(grads[:, :width], of_core(value_own, at, 0), NT)
            + dot(grads[:, width:], of_core(state_own, at, 0), NT)
            + dot(grads_other[:, :width], of_core(value_other, at, 0), NT)
            + dot(grads_other[:, width:], of_core(state_other, at, 0), NT)
        )

    input_grad = scatter(input_block)
    return (layer_output, input_grad)


def solution(mesh):
    split = Mesh(mesh.devices.reshape(4, 8, 4, 2), ("x", "z", "y", "c"))
    head = ("y", "c")
    in_specs = (
        P(SEQ, head),
        P(None, head),
        P(None, head),
        P(head, None),
        P(head, SEQ),
        P(head),
        P(SEQ, head),
    )
    return jax.shard_map(
        per_device,
        mesh=split,
        in_specs=in_specs,
        out_specs=(P(SEQ, head), P(SEQ, head)),
        check_vma=False,
    )
```

```python
import functools

import jax
import jax.numpy as jnp
from jax import lax
from jax.experimental import pallas as pl
from jax.experimental.pallas import tpu as pltpu
from jax.sharding import Mesh
from jax.sharding import PartitionSpec as P


STATE = 128
HEADS = 8
SEQ = ("x", "z")
F32 = jnp.float32
BF16 = jnp.bfloat16
NN = (((1,), (0,)), ((), ()))
NT = (((1,), (1,)), ((), ()))
TN = (((0,), (0,)), ((), ()))


def dot(a, b, dims):
    return lax.dot_general(a, b, dims, preferred_element_type=F32)


def spec(shape, kind=F32):
    return jax.ShapeDtypeStruct(shape, kind)


def call(body, outs, *args, flops=2**24, scratch=(), limit=24):
    moved = sum(a.size * a.dtype.itemsize for a in args)
    moved += sum(o.size * o.dtype.itemsize for o in outs)
    vmem = pl.BlockSpec(memory_space=pltpu.VMEM)
    return pl.pallas_call(
        body,
        out_shape=outs,
        in_specs=[vmem] * len(args),
        out_specs=[vmem] * len(outs),
        scratch_shapes=list(scratch),
        compiler_params=pltpu.CompilerParams(vmem_limit_bytes=limit * 2**20),
        cost_estimate=pl.CostEstimate(flops=flops, bytes_accessed=moved, transcendentals=0),
    )(*args)


def shift(array, axis, step):
    size = lax.axis_size(axis)
    return lax.ppermute(array, axis, [(i, (i + step) % size) for i in range(size)])


def parts_of(array):
    high = array.astype(BF16)
    rest = array - high.astype(F32)
    middle = rest.astype(BF16)
    return high, middle, (rest - middle.astype(F32)).astype(BF16)


def exact(parts, ones, dims, first):
    total = 0.0
    for part in parts:
        total = total + (dot(part, ones, dims) if first else dot(ones, part, dims))
    return total


def ones_where(keep):
    return jnp.where(keep, 1.0, 0.0).astype(BF16)


def iota(shape, dim):
    return lax.broadcasted_iota(jnp.int32, shape, dim)


def pair_lanes(array, two):
    shape = (array.shape[0], 128)
    low = jnp.broadcast_to(array[:, 2 * two : 2 * two + 1], shape)
    high = jnp.broadcast_to(array[:, 2 * two + 1 : 2 * two + 2], shape)
    return jnp.where(iota(shape, 1) < 64, low, high)


def inflow_of(decay):
    u = -2.0 * decay
    series = 1.0
    for k in (8, 7, 6, 5, 4, 3, 2):
        series = 1.0 - u * (1.0 / k) * series
    return jnp.sqrt(jnp.where(u < 0.5, u * series, 1.0 - jnp.exp(-u)))


def prepare_kernel(decay_ref, gain_ref, kernels, entering, to_end, totals, skip):
    decay = decay_ref[...]
    rows = decay.shape[1]
    square = (rows, rows)
    parts = parts_of(decay)
    row = exact(parts, ones_where(iota(square, 0) <= iota(square, 1)), NN, True)
    column = exact(parts, ones_where(iota(square, 1) <= iota(square, 0)), NT, False)
    decay_col = exact(parts, ones_where(iota(square, 1) == iota(square, 0)), NT, False)
    inflow_row = inflow_of(decay)
    causal = iota(square, 0) >= iota(square, 1)
    for h in range(HEADS):
        spread = jnp.where(causal, column[:, h : h + 1] - row[h : h + 1, :], -1e30)
        kernels[h] = (jnp.exp(spread) * inflow_row[h : h + 1, :]).astype(BF16)
    inflow_col = inflow_of(decay_col)
    total = column[rows - 1 : rows, :]
    total = jnp.broadcast_to(total, (8, HEADS))
    lanes = (HEADS, 128)
    spread = 0.0
    for k, part in enumerate(parts_of(total)):
        place = ones_where(iota(lanes, 1) == iota(lanes, 0) + HEADS * k)
        spread = spread + dot(part, place, NN)
    totals[...] = spread.astype(BF16)
    end = jnp.exp(total[0:1] - column) * inflow_col
    start = jnp.exp(column)
    for two in range(HEADS // 2):
        at = slice(two * 128, two * 128 + 128)
        entering[:, at] = pair_lanes(start, two)
        to_end[:, at] = pair_lanes(end, two)
        skip[:, at] = pair_lanes(gain_ref[...], two)


def weights_kernel(other, value_ref, state_ref, out_ref, value_to, state_to, out_to, sems):
    shard = value_to.shape[1]
    y, c = lax.axis_index("y"), lax.axis_index("c")
    core = 1 - c if other else c
    copies = []
    for k in range(4):
        at = pl.multiple_of((((y + k) % 4) * 2 + core) * shard, shard)
        copies.append((value_ref.at[pl.ds(at, shard), :], value_to.at[k]))
        copies.append((state_ref.at[pl.ds(at, shard), :], state_to.at[k]))
        copies.append((out_ref.at[:, pl.ds(at, shard)], out_to.at[k]))
    started = []
    for i, (source, target) in enumerate(copies):
        copy = pltpu.make_async_copy(source, target, sems.at[i])
        copy.start()
        started.append(copy)
    for copy in started:
        copy.wait()


def weights_of(other, value_weight, state_weight, output_weight, shard):
    width, pair = value_weight.shape[1], state_weight.shape[1]
    shapes = [(4, shard, width), (4, shard, pair), (4, width, shard)]
    return pl.pallas_call(
        functools.partial(weights_kernel, other),
        out_shape=[spec(s, BF16) for s in shapes],
        in_specs=[pl.BlockSpec(memory_space=pltpu.HBM)] * 3,
        out_specs=[pl.BlockSpec(memory_space=pltpu.VMEM)] * 3,
        scratch_shapes=[pltpu.SemaphoreType.DMA((12,))],
        compiler_params=pltpu.CompilerParams(vmem_limit_bytes=8 * 2**20),
        cost_estimate=pl.CostEstimate(flops=0, bytes_accessed=10 * 2**20, transcendentals=0),
    )(*[pltpu.with_memory_space_constraint(w, pltpu.HBM) for w in (value_weight, state_weight, output_weight)])


def input_first(
    own, low, high, value_a, state_a, value_b, state_b, own_ref, other_ref
):
    for value, state, out in ((value_b, state_b, other_ref), (value_a, state_a, own_ref)):
        width = value.shape[2]
        for weight, at in ((value, slice(0, width)), (state, slice(width, None))):
            out[:, at] = (
                dot(own[...], weight[0], NN)
                + dot(low[...], weight[3], NN)
                + dot(high[...], weight[1], NN)
            )


def input_last(
    far, value_a, state_a, value_b, state_b, own_sum, other_sum, own_ref, other_ref
):
    width = value_a.shape[2]
    for weight, at in ((value_b, slice(0, width)), (state_b, slice(width, None))):
        other_ref[:, at] = (other_sum[:, at] + dot(far[...], weight[2], NN)).astype(BF16)
    for weight, at in ((value_a, slice(0, width)), (state_a, slice(width, None))):
        own_ref[:, at] = own_sum[:, at] + dot(far[...], weight[2], NN)


def grad_first(own, low, high, out_a, out_b, own_ref, other_ref):
    for weight, out in ((out_b, other_ref), (out_a, own_ref)):
        out[...] = (
            dot(own[...], weight[0], NT)
            + dot(low[...], weight[3], NT)
            + dot(high[...], weight[1], NT)
        )


def grad_last(far, out_a, out_b, own_sum, other_sum, own_ref, other_ref):
    other_ref[...] = (other_sum[...] + dot(far[...], out_b[2], NT)).astype(BF16)
    own_ref[...] = own_sum[...] + dot(far[...], out_a[2], NT)


def masked(pair, odd):
    lane = iota(pair.shape, 1)
    keep = lane >= 64 if odd else lane < 64
    return jnp.where(keep, pair, jnp.zeros_like(pair))


def mix_kernel(
    input_sum,
    input_other,
    to_end,
    decay_ref,
    skip_ref,
    mix_ref,
    end_ref,
    local_ref,
    weight_ref,
):
    width = local_ref.shape[1]
    mix = (input_sum[...] + input_other[...].astype(F32)).astype(BF16)
    mix_ref[...] = mix
    writer = mix[:, width : width + STATE]
    reader = mix[:, width + STATE :]
    scaled = (mix[:, :width].astype(F32) * to_end[...]).astype(BF16)
    end_ref[...] = dot(writer, scaled, TN).astype(BF16)
    scores = dot(reader, writer, NT)
    for two in range(HEADS // 2):
        at = slice(two * 128, two * 128 + 128)
        value_pair = mix[:, at]
        local = value_pair.astype(F32) * skip_ref[:, at]
        for odd in range(2):
            h = 2 * two + odd
            weight = (scores * decay_ref[h].astype(F32)).astype(BF16)
            weight_ref[h] = weight
            local = local + dot(weight, masked(value_pair, odd), NN)
        local_ref[:, at] = local


def state_kernel(mix_ref, grad_sum, grad_other, entering, end_ref, totals, grad_ref, pay_ref):
    width = grad_sum.shape[1]
    grad = (grad_sum[...] + grad_other[...].astype(F32)).astype(BF16)
    grad_ref[...] = grad
    scaled = (grad.astype(F32) * entering[...]).astype(BF16)
    reader = mix_ref[:, width + STATE :]
    pay_ref[:STATE, :width] = end_ref[...]
    pay_ref[STATE:, :width] = dot(reader, scaled, TN).astype(BF16)
    total = totals[0:1, :].astype(F32)
    pay_ref[:, width:] = jnp.broadcast_to(total, (2 * STATE, 128)).astype(BF16)


def owner_kernel(pieces_ref, out_ref, decay_ref):
    count, width = out_ref.shape[0], out_ref.shape[2]
    lanes = (128, width)
    head = iota(lanes, 1) // 64
    place = iota(lanes, 0)
    keep = (place % HEADS == head) & (place < 3 * HEADS)
    totals = pieces_ref[:, 0, width:]
    decay_ref[...] = jnp.exp(dot(totals, ones_where(keep), NN))
    back = lax.axis_index("x") >= 2
    state = jnp.zeros(out_ref.shape[1:], F32)
    for k in range(count):
        at = jnp.where(back, count - 1 - k, k)
        out_ref[at] = state.astype(BF16)
        state = state * decay_ref[pl.ds(at, 1), :] + pieces_ref[at, :, :width].astype(F32)


def output_kernel(mix_ref, states_ref, entering, local_ref, out_ref):
    width = local_ref.shape[1]
    reader = mix_ref[:, width + STATE :]
    mixed = local_ref[...] + dot(reader, states_ref[:STATE, :], NN) * entering[...]
    out_ref[...] = mixed.astype(BF16)


def gradient_kernel(
    mix_ref, grad_ref, states_ref, entering, to_end, skip_ref, weight_ref, decay_ref, out_ref
):
    rows, width = grad_ref.shape
    writer = mix_ref[:, width : width + STATE]
    reader = mix_ref[:, width + STATE :]
    incoming = states_ref[:STATE, :]
    outgoing = states_ref[STATE:, :]
    score_grad = jnp.zeros((rows, rows), F32)
    for two in range(HEADS // 2):
        at = slice(two * 128, two * 128 + 128)
        value_pair = mix_ref[:, at]
        grad_pair = grad_ref[:, at]
        back = grad_pair.astype(F32) * skip_ref[:, at]
        back = back + dot(writer, outgoing[:, at], NN) * to_end[:, at]
        for odd in range(2):
            h = 2 * two + odd
            grad_one = masked(grad_pair, odd)
            back = back + dot(weight_ref[h], grad_one, TN)
            score_grad = score_grad + dot(grad_one, value_pair, NT) * decay_ref[h].astype(F32)
        out_ref[:, at] = back.astype(BF16)
    score_grad = score_grad.astype(BF16)
    value_scaled = (mix_ref[:, :width].astype(F32) * to_end[...]).astype(BF16)
    write = dot(score_grad, reader, TN) + dot(value_scaled, outgoing, NT)
    out_ref[:, width : width + STATE] = write.astype(BF16)
    grad_scaled = (grad_ref[...].astype(F32) * entering[...]).astype(BF16)
    read = dot(score_grad, writer, NN) + dot(grad_scaled, incoming, NT)
    out_ref[:, width + STATE :] = read.astype(BF16)


def output_blocks(blocks, fin, other, weight_a, weight_b, *outs):
    for out, k in zip(outs, blocks):
        total = dot(fin[...], weight_a[k], NN) + dot(other[...], weight_b[k], NN)
        out[...] = total.astype(out.dtype)


def input_blocks(blocks, fin, other, value_a, state_a, value_b, state_b, *outs):
    width = value_a.shape[2]
    for out, k in zip(outs, blocks):
        total = (
            dot(fin[:, :width], value_a[k], NT)
            + dot(fin[:, width:], state_a[k], NT)
            + dot(other[:, :width], value_b[k], NT)
            + dot(other[:, width:], state_b[k], NT)
        )
        out[...] = total.astype(out.dtype)


def add_kernel(groups, *refs):
    outs = refs[-groups:]
    count = (len(refs) - groups) // groups
    for g, out in enumerate(outs):
        total = refs[g * count][...].astype(F32)
        for ref in refs[g * count + 1 : (g + 1) * count]:
            total = total + ref[...].astype(F32)
        out[...] = total.astype(out.dtype)


def per_device(
    layer_input, value_weight, state_weight, output_weight, log_decay, skip_gain, output_grad
):
    rows, shard = layer_input.shape
    width, pair = value_weight.shape[1], state_weight.shape[1]
    wide = spec((rows, width))
    both = spec((rows, width + pair))
    block = spec((rows, shard))
    block_low = spec((rows, shard), BF16)

    input_low = shift(layer_input, "y", 1)
    input_high = shift(layer_input, "y", -1)
    grad_high = shift(output_grad, "y", -1)
    input_far = shift(input_low, "y", 1)
    grad_low = shift(output_grad, "y", 1)
    grad_far = shift(grad_high, "y", -1)

    sent = weights_of(True, value_weight, state_weight, output_weight, shard)
    value_b, state_b, out_b = [shift(w, "c", 1) for w in sent]
    value_a, state_a, out_a = weights_of(False, value_weight, state_weight, output_weight, shard)

    square = spec((HEADS, rows, rows), BF16)
    decays, entering, to_end, totals, skip = call(
        prepare_kernel,
        [square, wide, wide, spec((8, 128), BF16), spec((1, width))],
        log_decay,
        skip_gain.reshape(1, HEADS),
    )

    input_weights = (value_a, state_a, value_b, state_b)
    sums = call(
        input_first, [both, both], layer_input, input_low, input_high, *input_weights, flops=2**30
    )
    input_sum, input_send = call(
        input_last, [both, spec(both.shape, BF16)], input_far, *input_weights, *sums, flops=2**29
    )
    input_other = shift(input_send, "c", 1)
    mix, end, local, weights = call(
        mix_kernel,
        [spec((rows, width + pair), BF16), spec((STATE, width), BF16), wide, square],
        input_sum,
        input_other,
        to_end,
        decays,
        skip,
        flops=2**28,
    )
    sums = call(
        grad_first, [wide, wide], output_grad, grad_low, grad_high, out_a, out_b, flops=2**30
    )
    grad_sum, grad_send = call(
        grad_last, [wide, spec(wide.shape, BF16)], grad_far, out_a, out_b, *sums, flops=2**29
    )
    grad_other = shift(grad_send, "c", 1)
    grad, pay = call(
        state_kernel,
        [spec((rows, width), BF16), spec((2 * STATE, width + 128), BF16)],
        mix,
        grad_sum,
        grad_other,
        entering,
        end,
        totals,
    )
    pay, local = lax.optimization_barrier((pay, local))
    arrived = lax.all_to_all(pay.reshape(32, 8, width + 128), SEQ, 0, 0, tiled=True)
    owned = call(
        owner_kernel, [spec((32, 8, width), BF16)], arrived, scratch=[pltpu.VMEM((32, width), F32)]
    )[0]
    states = lax.all_to_all(owned, SEQ, 0, 0, tiled=True).reshape(2 * STATE, width)

    mixed = call(
        output_kernel, [spec((rows, width), BF16)], mix, states, entering, local, flops=2**25
    )[0]
    mixed_other = shift(mixed, "c", 1)
    grads = call(
        gradient_kernel,
        [spec((rows, width + pair), BF16)],
        mix,
        grad,
        states,
        entering,
        to_end,
        skip,
        weights,
        decays,
        flops=2**28,
    )[0]
    grads_other = shift(grads, "c", 1)

    def outputs(blocks, kinds):
        return call(
            functools.partial(output_blocks, blocks),
            kinds,
            mixed,
            mixed_other,
            out_a,
            out_b,
            flops=2**28 * len(blocks),
        )

    def inputs(blocks, kinds):
        return call(
            functools.partial(input_blocks, blocks),
            kinds,
            grads,
            grads_other,
            *input_weights,
            flops=2**28 * len(blocks),
        )

    add = functools.partial(add_kernel, 1)
    (out_2,) = outputs((2,), [block_low])
    out_from = shift(out_2, "y", 1)
    (in_2,) = inputs((2,), [block_low])
    in_from = shift(in_2, "y", -1)
    (out_3,) = outputs((3,), [block_low])
    out_high = shift(out_3, "y", -1)
    (in_1,) = inputs((1,), [block_low])
    in_low = shift(in_1, "y", 1)
    out_1, out_0 = outputs((1, 0), [block] * 2)
    in_3, in_0 = inputs((3, 0), [block] * 2)
    out_1 = call(add, [block_low], out_1, out_from)[0]
    out_low = shift(out_1, "y", 1)
    in_3 = call(add, [block_low], in_3, in_from)[0]
    in_high = shift(in_3, "y", -1)
    layer_output = call(add, [block_low], out_0, out_high, out_low)[0]
    input_grad = call(add, [block_low], in_0, in_low, in_high)[0]
    return (layer_output, input_grad)


def solution(mesh):
    split = Mesh(mesh.devices.reshape(4, 8, 4, 2), ("x", "z", "y", "c"))
    head = ("y", "c")
    in_specs = (
        P(SEQ, head),
        P(None, head),
        P(None, head),
        P(head, None),
        P(head, SEQ),
        P(head),
        P(SEQ, head),
    )
    return jax.shard_map(
        per_device,
        mesh=split,
        in_specs=in_specs,
        out_specs=(P(SEQ, head), P(SEQ, head)),
        check_vma=False,
    )
```

```python
import functools

import jax
import jax.numpy as jnp
from jax import lax
from jax.experimental import pallas as pl
from jax.experimental.pallas import tpu as pltpu
from jax.sharding import Mesh
from jax.sharding import PartitionSpec as P


STATE = 128
HEADS = 8
SEQ = ("x", "z")
F32 = jnp.float32
BF16 = jnp.bfloat16
NN = (((1,), (0,)), ((), ()))
NT = (((1,), (1,)), ((), ()))
TN = (((0,), (0,)), ((), ()))


def dot(a, b, dims):
    return lax.dot_general(a, b, dims, preferred_element_type=F32)


def spec(shape, kind=F32):
    return jax.ShapeDtypeStruct(shape, kind)


def call(body, outs, *args, flops=2**24, scratch=(), limit=24):
    moved = sum(a.size * a.dtype.itemsize for a in args)
    moved += sum(o.size * o.dtype.itemsize for o in outs)
    vmem = pl.BlockSpec(memory_space=pltpu.VMEM)
    return pl.pallas_call(
        body,
        out_shape=outs,
        in_specs=[vmem] * len(args),
        out_specs=[vmem] * len(outs),
        scratch_shapes=list(scratch),
        compiler_params=pltpu.CompilerParams(vmem_limit_bytes=limit * 2**20),
        cost_estimate=pl.CostEstimate(flops=flops, bytes_accessed=moved, transcendentals=0),
    )(*args)


def shift(array, axis, step):
    size = lax.axis_size(axis)
    return lax.ppermute(array, axis, [(i, (i + step) % size) for i in range(size)])


def ring(array, sign):
    pairs = []
    for y in range(4):
        for c in range(2):
            step = sign * (1 - 2 * c)
            pairs.append((2 * y + c, 2 * ((y + step) % 4) + c))
    return lax.ppermute(array, ("y", "c"), pairs)


def parts_of(array):
    high = array.astype(BF16)
    rest = array - high.astype(F32)
    middle = rest.astype(BF16)
    return high, middle, (rest - middle.astype(F32)).astype(BF16)


def exact(parts, ones, dims, first):
    total = 0.0
    for part in parts:
        total = total + (dot(part, ones, dims) if first else dot(ones, part, dims))
    return total


def ones_where(keep):
    return jnp.where(keep, 1.0, 0.0).astype(BF16)


def iota(shape, dim):
    return lax.broadcasted_iota(jnp.int32, shape, dim)


def pair_lanes(array, two):
    shape = (array.shape[0], 128)
    low = jnp.broadcast_to(array[:, 2 * two : 2 * two + 1], shape)
    high = jnp.broadcast_to(array[:, 2 * two + 1 : 2 * two + 2], shape)
    return jnp.where(iota(shape, 1) < 64, low, high)


def inflow_of(decay):
    u = -2.0 * decay
    series = 1.0
    for k in (8, 7, 6, 5, 4, 3, 2):
        series = 1.0 - u * (1.0 / k) * series
    return jnp.sqrt(jnp.where(u < 0.5, u * series, 1.0 - jnp.exp(-u)))


def prepare_kernel(decay_ref, gain_ref, kernels, entering, to_end, totals, skip):
    decay = decay_ref[...]
    rows = decay.shape[1]
    square = (rows, rows)
    parts = parts_of(decay)
    row = exact(parts, ones_where(iota(square, 0) <= iota(square, 1)), NN, True)
    column = exact(parts, ones_where(iota(square, 1) <= iota(square, 0)), NT, False)
    decay_col = exact(parts, ones_where(iota(square, 1) == iota(square, 0)), NT, False)
    inflow_row = inflow_of(decay)
    causal = iota(square, 0) >= iota(square, 1)
    for h in range(HEADS):
        spread = jnp.where(causal, column[:, h : h + 1] - row[h : h + 1, :], -1e30)
        kernels[h] = (jnp.exp(spread) * inflow_row[h : h + 1, :]).astype(BF16)
    inflow_col = inflow_of(decay_col)
    total = column[rows - 1 : rows, :]
    total = jnp.broadcast_to(total, (8, HEADS))
    lanes = (HEADS, 128)
    spread = 0.0
    for k, part in enumerate(parts_of(total)):
        place = ones_where(iota(lanes, 1) == iota(lanes, 0) + HEADS * k)
        spread = spread + dot(part, place, NN)
    totals[...] = spread.astype(BF16)
    end = jnp.exp(total[0:1] - column) * inflow_col
    start = jnp.exp(column)
    for two in range(HEADS // 2):
        at = slice(two * 128, two * 128 + 128)
        entering[:, at] = pair_lanes(start, two)
        to_end[:, at] = pair_lanes(end, two)
        skip[:, at] = pair_lanes(gain_ref[...], two)


def weights_kernel(other, value_ref, state_ref, out_ref, value_to, state_to, out_to, sems):
    shard = value_to.shape[1]
    y, c = lax.axis_index("y"), lax.axis_index("c")
    core = 1 - c if other else c
    copies = []
    for k in range(4):
        at = pl.multiple_of((((y + k) % 4) * 2 + core) * shard, shard)
        copies.append((value_ref.at[pl.ds(at, shard), :], value_to.at[k]))
        copies.append((state_ref.at[pl.ds(at, shard), :], state_to.at[k]))
        copies.append((out_ref.at[:, pl.ds(at, shard)], out_to.at[k]))
    started = []
    for i, (source, target) in enumerate(copies):
        copy = pltpu.make_async_copy(source, target, sems.at[i])
        copy.start()
        started.append(copy)
    for copy in started:
        copy.wait()


def weights_of(other, value_weight, state_weight, output_weight, shard):
    width, pair = value_weight.shape[1], state_weight.shape[1]
    shapes = [(4, shard, width), (4, shard, pair), (4, width, shard)]
    return pl.pallas_call(
        functools.partial(weights_kernel, other),
        out_shape=[spec(s, BF16) for s in shapes],
        in_specs=[pl.BlockSpec(memory_space=pltpu.HBM)] * 3,
        out_specs=[pl.BlockSpec(memory_space=pltpu.VMEM)] * 3,
        scratch_shapes=[pltpu.SemaphoreType.DMA((12,))],
        compiler_params=pltpu.CompilerParams(vmem_limit_bytes=8 * 2**20),
        cost_estimate=pl.CostEstimate(flops=0, bytes_accessed=10 * 2**20, transcendentals=0),
    )(*[pltpu.with_memory_space_constraint(w, pltpu.HBM) for w in (value_weight, state_weight, output_weight)])


def input_first(
    own, low, high, value_a, state_a, value_b, state_b, own_ref, other_ref
):
    for value, state, out in ((value_b, state_b, other_ref), (value_a, state_a, own_ref)):
        width = value.shape[2]
        for weight, at in ((value, slice(0, width)), (state, slice(width, None))):
            out[:, at] = (
                dot(own[...], weight[0], NN)
                + dot(low[...], weight[3], NN)
                + dot(high[...], weight[1], NN)
            )


def input_last(
    far, value_a, state_a, value_b, state_b, own_sum, other_sum, own_ref, other_ref
):
    width = value_a.shape[2]
    for weight, at in ((value_b, slice(0, width)), (state_b, slice(width, None))):
        other_ref[:, at] = (other_sum[:, at] + dot(far[...], weight[2], NN)).astype(BF16)
    for weight, at in ((value_a, slice(0, width)), (state_a, slice(width, None))):
        own_ref[:, at] = own_sum[:, at] + dot(far[...], weight[2], NN)


def grad_first(own, low, high, out_a, out_b, own_ref, other_ref):
    for weight, out in ((out_b, other_ref), (out_a, own_ref)):
        out[...] = (
            dot(own[...], weight[0], NT)
            + dot(low[...], weight[3], NT)
            + dot(high[...], weight[1], NT)
        )


def grad_last(far, out_a, out_b, own_sum, other_sum, own_ref, other_ref):
    other_ref[...] = (other_sum[...] + dot(far[...], out_b[2], NT)).astype(BF16)
    own_ref[...] = own_sum[...] + dot(far[...], out_a[2], NT)


def masked(pair, odd):
    lane = iota(pair.shape, 1)
    keep = lane >= 64 if odd else lane < 64
    return jnp.where(keep, pair, jnp.zeros_like(pair))


def mix_kernel(
    input_sum,
    input_other,
    to_end,
    decay_ref,
    skip_ref,
    mix_ref,
    end_ref,
    local_ref,
    weight_ref,
):
    width = local_ref.shape[1]
    mix = (input_sum[...] + input_other[...].astype(F32)).astype(BF16)
    mix_ref[...] = mix
    writer = mix[:, width : width + STATE]
    reader = mix[:, width + STATE :]
    scaled = (mix[:, :width].astype(F32) * to_end[...]).astype(BF16)
    end_ref[...] = dot(writer, scaled, TN).astype(BF16)
    scores = dot(reader, writer, NT)
    for two in range(HEADS // 2):
        at = slice(two * 128, two * 128 + 128)
        value_pair = mix[:, at]
        local = value_pair.astype(F32) * skip_ref[:, at]
        for odd in range(2):
            h = 2 * two + odd
            weight = (scores * decay_ref[h].astype(F32)).astype(BF16)
            weight_ref[h] = weight
            local = local + dot(weight, masked(value_pair, odd), NN)
        local_ref[:, at] = local


def state_kernel(mix_ref, grad_sum, grad_other, entering, end_ref, totals, grad_ref, pay_ref):
    width = grad_sum.shape[1]
    grad = (grad_sum[...] + grad_other[...].astype(F32)).astype(BF16)
    grad_ref[...] = grad
    scaled = (grad.astype(F32) * entering[...]).astype(BF16)
    reader = mix_ref[:, width + STATE :]
    pay_ref[:STATE, :width] = end_ref[...]
    pay_ref[STATE:, :width] = dot(reader, scaled, TN).astype(BF16)
    total = totals[0:1, :].astype(F32)
    pay_ref[:, width:] = jnp.broadcast_to(total, (2 * STATE, 128)).astype(BF16)


def owner_kernel(pieces_ref, out_ref, decay_ref):
    count, width = out_ref.shape[0], out_ref.shape[2]
    lanes = (128, width)
    head = iota(lanes, 1) // 64
    place = iota(lanes, 0)
    keep = (place % HEADS == head) & (place < 3 * HEADS)
    totals = pieces_ref[:, 0, width:]
    decay_ref[...] = jnp.exp(dot(totals, ones_where(keep), NN))
    back = lax.axis_index("x") >= 2
    state = jnp.zeros(out_ref.shape[1:], F32)
    for k in range(count):
        at = jnp.where(back, count - 1 - k, k)
        out_ref[at] = state.astype(BF16)
        state = state * decay_ref[pl.ds(at, 1), :] + pieces_ref[at, :, :width].astype(F32)


def output_kernel(mix_ref, states_ref, entering, local_ref, out_ref):
    width = local_ref.shape[1]
    reader = mix_ref[:, width + STATE :]
    mixed = local_ref[...] + dot(reader, states_ref[:STATE, :], NN) * entering[...]
    out_ref[...] = mixed.astype(BF16)


def gradient_kernel(
    mix_ref, grad_ref, states_ref, entering, to_end, skip_ref, weight_ref, decay_ref, out_ref
):
    rows, width = grad_ref.shape
    writer = mix_ref[:, width : width + STATE]
    reader = mix_ref[:, width + STATE :]
    incoming = states_ref[:STATE, :]
    outgoing = states_ref[STATE:, :]
    score_grad = jnp.zeros((rows, rows), F32)
    for two in range(HEADS // 2):
        at = slice(two * 128, two * 128 + 128)
        value_pair = mix_ref[:, at]
        grad_pair = grad_ref[:, at]
        back = grad_pair.astype(F32) * skip_ref[:, at]
        back = back + dot(writer, outgoing[:, at], NN) * to_end[:, at]
        for odd in range(2):
            h = 2 * two + odd
            grad_one = masked(grad_pair, odd)
            back = back + dot(weight_ref[h], grad_one, TN)
            score_grad = score_grad + dot(grad_one, value_pair, NT) * decay_ref[h].astype(F32)
        out_ref[:, at] = back.astype(BF16)
    score_grad = score_grad.astype(BF16)
    value_scaled = (mix_ref[:, :width].astype(F32) * to_end[...]).astype(BF16)
    write = dot(score_grad, reader, TN) + dot(value_scaled, outgoing, NT)
    out_ref[:, width : width + STATE] = write.astype(BF16)
    grad_scaled = (grad_ref[...].astype(F32) * entering[...]).astype(BF16)
    read = dot(score_grad, writer, NN) + dot(grad_scaled, incoming, NT)
    out_ref[:, width + STATE :] = read.astype(BF16)


def resolved(block):
    c = lax.axis_index("c")
    return {"A": 3 - 2 * c, "B": 1 + 2 * c}.get(block, block)


def output_blocks(blocks, fin, other, weight_a, weight_b, *outs):
    for out, block in zip(outs, blocks):
        k = resolved(block)
        total = dot(fin[...], weight_a[k], NN) + dot(other[...], weight_b[k], NN)
        out[...] = total.astype(out.dtype)


def input_blocks(blocks, fin, other, value_a, state_a, value_b, state_b, *outs):
    width = value_a.shape[2]
    for out, block in zip(outs, blocks):
        k = resolved(block)
        total = (
            dot(fin[:, :width], value_a[k], NT)
            + dot(fin[:, width:], state_a[k], NT)
            + dot(other[:, :width], value_b[k], NT)
            + dot(other[:, width:], state_b[k], NT)
        )
        out[...] = total.astype(out.dtype)


def add_kernel(groups, *refs):
    outs = refs[-groups:]
    count = (len(refs) - groups) // groups
    for g, out in enumerate(outs):
        total = refs[g * count][...].astype(F32)
        for ref in refs[g * count + 1 : (g + 1) * count]:
            total = total + ref[...].astype(F32)
        out[...] = total.astype(out.dtype)


def per_device(
    layer_input, value_weight, state_weight, output_weight, log_decay, skip_gain, output_grad
):
    rows, shard = layer_input.shape
    width, pair = value_weight.shape[1], state_weight.shape[1]
    wide = spec((rows, width))
    both = spec((rows, width + pair))
    block = spec((rows, shard))
    block_low = spec((rows, shard), BF16)

    input_low = shift(layer_input, "y", 1)
    input_high = shift(layer_input, "y", -1)
    grad_high = shift(output_grad, "y", -1)
    input_far = shift(input_low, "y", 1)
    grad_low = shift(output_grad, "y", 1)
    grad_far = shift(grad_high, "y", -1)

    sent = weights_of(True, value_weight, state_weight, output_weight, shard)
    value_b, state_b, out_b = [shift(w, "c", 1) for w in sent]
    value_a, state_a, out_a = weights_of(False, value_weight, state_weight, output_weight, shard)

    square = spec((HEADS, rows, rows), BF16)
    decays, entering, to_end, totals, skip = call(
        prepare_kernel,
        [square, wide, wide, spec((8, 128), BF16), spec((1, width))],
        log_decay,
        skip_gain.reshape(1, HEADS),
    )

    input_weights = (value_a, state_a, value_b, state_b)
    sums = call(
        input_first, [both, both], layer_input, input_low, input_high, *input_weights, flops=2**30
    )
    input_sum, input_send = call(
        input_last, [both, spec(both.shape, BF16)], input_far, *input_weights, *sums, flops=2**29
    )
    input_other = shift(input_send, "c", 1)
    mix, end, local, weights = call(
        mix_kernel,
        [spec((rows, width + pair), BF16), spec((STATE, width), BF16), wide, square],
        input_sum,
        input_other,
        to_end,
        decays,
        skip,
        flops=2**28,
    )
    sums = call(
        grad_first, [wide, wide], output_grad, grad_low, grad_high, out_a, out_b, flops=2**30
    )
    grad_sum, grad_send = call(
        grad_last, [wide, spec(wide.shape, BF16)], grad_far, out_a, out_b, *sums, flops=2**29
    )
    grad_other = shift(grad_send, "c", 1)
    grad, pay = call(
        state_kernel,
        [spec((rows, width), BF16), spec((2 * STATE, width + 128), BF16)],
        mix,
        grad_sum,
        grad_other,
        entering,
        end,
        totals,
    )
    pay, local = lax.optimization_barrier((pay, local))
    arrived = lax.all_to_all(pay.reshape(32, 8, width + 128), SEQ, 0, 0, tiled=True)
    owned = call(
        owner_kernel, [spec((32, 8, width), BF16)], arrived, scratch=[pltpu.VMEM((32, width), F32)]
    )[0]
    states = lax.all_to_all(owned, SEQ, 0, 0, tiled=True).reshape(2 * STATE, width)

    mixed = call(
        output_kernel, [spec((rows, width), BF16)], mix, states, entering, local, flops=2**25
    )[0]
    mixed_other = shift(mixed, "c", 1)
    grads = call(
        gradient_kernel,
        [spec((rows, width + pair), BF16)],
        mix,
        grad,
        states,
        entering,
        to_end,
        skip,
        weights,
        decays,
        flops=2**28,
    )[0]
    grads_other = shift(grads, "c", 1)

    def outputs(blocks, kinds):
        return call(
            functools.partial(output_blocks, blocks),
            kinds,
            mixed,
            mixed_other,
            out_a,
            out_b,
            flops=2**28 * len(blocks),
        )

    def inputs(blocks, kinds):
        return call(
            functools.partial(input_blocks, blocks),
            kinds,
            grads,
            grads_other,
            *input_weights,
            flops=2**28 * len(blocks),
        )

    add = functools.partial(add_kernel, 1)
    (out_2,) = outputs((2,), [block_low])
    out_from = ring(out_2, 1)
    (in_2,) = inputs((2,), [block_low])
    in_from = ring(in_2, 1)
    (out_a_block,) = outputs(("A",), [block_low])
    out_near = ring(out_a_block, -1)
    (in_a_block,) = inputs(("A",), [block_low])
    in_near = ring(in_a_block, -1)
    out_b_block, out_0 = outputs(("B", 0), [block] * 2)
    in_b_block, in_0 = inputs(("B", 0), [block] * 2)
    out_b_block = call(add, [block_low], out_b_block, out_from)[0]
    out_last = ring(out_b_block, 1)
    in_b_block = call(add, [block_low], in_b_block, in_from)[0]
    in_last = ring(in_b_block, 1)
    layer_output = call(add, [block_low], out_0, out_near, out_last)[0]
    input_grad = call(add, [block_low], in_0, in_near, in_last)[0]
    return (layer_output, input_grad)


def solution(mesh):
    split = Mesh(mesh.devices.reshape(4, 8, 4, 2), ("x", "z", "y", "c"))
    head = ("y", "c")
    in_specs = (
        P(SEQ, head),
        P(None, head),
        P(None, head),
        P(head, None),
        P(head, SEQ),
        P(head),
        P(SEQ, head),
    )
    return jax.shard_map(
        per_device,
        mesh=split,
        in_specs=in_specs,
        out_specs=(P(SEQ, head), P(SEQ, head)),
        check_vma=False,
    )
```

```python
import functools

import jax
import jax.numpy as jnp
from jax import lax
from jax.experimental import pallas as pl
from jax.experimental.pallas import tpu as pltpu
from jax.sharding import Mesh
from jax.sharding import PartitionSpec as P


STATE = 128
HEADS = 8
SEQ = ("x", "z")
F32 = jnp.float32
BF16 = jnp.bfloat16
NN = (((1,), (0,)), ((), ()))
NT = (((1,), (1,)), ((), ()))
TN = (((0,), (0,)), ((), ()))


def dot(a, b, dims):
    return lax.dot_general(a, b, dims, preferred_element_type=F32)


def spec(shape, kind=F32):
    return jax.ShapeDtypeStruct(shape, kind)


def call(body, outs, *args, flops=2**24, scratch=(), limit=24):
    moved = sum(a.size * a.dtype.itemsize for a in args)
    moved += sum(o.size * o.dtype.itemsize for o in outs)
    vmem = pl.BlockSpec(memory_space=pltpu.VMEM)
    return pl.pallas_call(
        body,
        out_shape=outs,
        in_specs=[vmem] * len(args),
        out_specs=[vmem] * len(outs),
        scratch_shapes=list(scratch),
        compiler_params=pltpu.CompilerParams(vmem_limit_bytes=limit * 2**20),
        cost_estimate=pl.CostEstimate(flops=flops, bytes_accessed=moved, transcendentals=0),
    )(*args)


def shift(array, axis, step):
    size = lax.axis_size(axis)
    return lax.ppermute(array, axis, [(i, (i + step) % size) for i in range(size)])


def ring(array, sign):
    pairs = []
    for y in range(4):
        for c in range(2):
            step = sign * (1 - 2 * c)
            pairs.append((2 * y + c, 2 * ((y + step) % 4) + c))
    return lax.ppermute(array, ("y", "c"), pairs)


def parts_of(array):
    high = array.astype(BF16)
    rest = array - high.astype(F32)
    middle = rest.astype(BF16)
    return high, middle, (rest - middle.astype(F32)).astype(BF16)


def exact(parts, ones, dims, first):
    total = 0.0
    for part in parts:
        total = total + (dot(part, ones, dims) if first else dot(ones, part, dims))
    return total


def ones_where(keep):
    return jnp.where(keep, 1.0, 0.0).astype(BF16)


def iota(shape, dim):
    return lax.broadcasted_iota(jnp.int32, shape, dim)


def pair_lanes(array, two):
    shape = (array.shape[0], 128)
    low = jnp.broadcast_to(array[:, 2 * two : 2 * two + 1], shape)
    high = jnp.broadcast_to(array[:, 2 * two + 1 : 2 * two + 2], shape)
    return jnp.where(iota(shape, 1) < 64, low, high)


def inflow_of(decay):
    u = -2.0 * decay
    series = 1.0
    for k in (8, 7, 6, 5, 4, 3, 2):
        series = 1.0 - u * (1.0 / k) * series
    return jnp.sqrt(jnp.where(u < 0.5, u * series, 1.0 - jnp.exp(-u)))


def prepare_kernel(decay_ref, gain_ref, kernels, entering, to_end, totals, skip):
    decay = decay_ref[...]
    rows = decay.shape[1]
    square = (rows, rows)
    parts = parts_of(decay)
    row = exact(parts, ones_where(iota(square, 0) <= iota(square, 1)), NN, True)
    column = exact(parts, ones_where(iota(square, 1) <= iota(square, 0)), NT, False)
    decay_col = exact(parts, ones_where(iota(square, 1) == iota(square, 0)), NT, False)
    inflow_row = inflow_of(decay)
    causal = iota(square, 0) >= iota(square, 1)
    for h in range(HEADS):
        spread = jnp.where(causal, column[:, h : h + 1] - row[h : h + 1, :], -1e30)
        kernels[h] = (jnp.exp(spread) * inflow_row[h : h + 1, :]).astype(BF16)
    inflow_col = inflow_of(decay_col)
    total = column[rows - 1 : rows, :]
    total = jnp.broadcast_to(total, (8, HEADS))
    lanes = (HEADS, 128)
    spread = 0.0
    for k, part in enumerate(parts_of(total)):
        place = ones_where(iota(lanes, 1) == iota(lanes, 0) + HEADS * k)
        spread = spread + dot(part, place, NN)
    totals[...] = spread.astype(BF16)
    end = jnp.exp(total[0:1] - column) * inflow_col
    start = jnp.exp(column)
    for two in range(HEADS // 2):
        at = slice(two * 128, two * 128 + 128)
        entering[:, at] = pair_lanes(start, two)
        to_end[:, at] = pair_lanes(end, two)
        skip[:, at] = pair_lanes(gain_ref[...], two)


def weights_kernel(other, value_ref, state_ref, out_ref, value_to, state_to, out_to, sems):
    shard = value_to.shape[1]
    y, c = lax.axis_index("y"), lax.axis_index("c")
    core = 1 - c if other else c
    copies = []
    for k in range(4):
        at = pl.multiple_of((((y + k) % 4) * 2 + core) * shard, shard)
        copies.append((value_ref.at[pl.ds(at, shard), :], value_to.at[k]))
        copies.append((state_ref.at[pl.ds(at, shard), :], state_to.at[k]))
        copies.append((out_ref.at[:, pl.ds(at, shard)], out_to.at[k]))
    started = []
    for i, (source, target) in enumerate(copies):
        copy = pltpu.make_async_copy(source, target, sems.at[i])
        copy.start()
        started.append(copy)
    for copy in started:
        copy.wait()


def weights_of(other, value_weight, state_weight, output_weight, shard):
    width, pair = value_weight.shape[1], state_weight.shape[1]
    shapes = [(4, shard, width), (4, shard, pair), (4, width, shard)]
    return pl.pallas_call(
        functools.partial(weights_kernel, other),
        out_shape=[spec(s, BF16) for s in shapes],
        in_specs=[pl.BlockSpec(memory_space=pltpu.HBM)] * 3,
        out_specs=[pl.BlockSpec(memory_space=pltpu.VMEM)] * 3,
        scratch_shapes=[pltpu.SemaphoreType.DMA((12,))],
        compiler_params=pltpu.CompilerParams(vmem_limit_bytes=8 * 2**20),
        cost_estimate=pl.CostEstimate(flops=0, bytes_accessed=10 * 2**20, transcendentals=0),
    )(*[pltpu.with_memory_space_constraint(w, pltpu.HBM) for w in (value_weight, state_weight, output_weight)])


def input_first(
    own, low, high, value_a, state_a, value_b, state_b, own_ref, other_ref
):
    for value, state, out in ((value_b, state_b, other_ref), (value_a, state_a, own_ref)):
        width = value.shape[2]
        for weight, at in ((value, slice(0, width)), (state, slice(width, None))):
            out[:, at] = (
                dot(own[...], weight[0], NN)
                + dot(low[...], weight[3], NN)
                + dot(high[...], weight[1], NN)
            )


def input_last(
    far, value_a, state_a, value_b, state_b, own_sum, other_sum, own_ref, other_ref
):
    width = value_a.shape[2]
    for weight, at in ((value_b, slice(0, width)), (state_b, slice(width, None))):
        other_ref[:, at] = (other_sum[:, at] + dot(far[...], weight[2], NN)).astype(BF16)
    for weight, at in ((value_a, slice(0, width)), (state_a, slice(width, None))):
        own_ref[:, at] = own_sum[:, at] + dot(far[...], weight[2], NN)


def grad_first(own, low, high, out_a, out_b, own_ref, other_ref):
    for weight, out in ((out_b, other_ref), (out_a, own_ref)):
        out[...] = (
            dot(own[...], weight[0], NT)
            + dot(low[...], weight[3], NT)
            + dot(high[...], weight[1], NT)
        )


def grad_last(far, out_a, out_b, own_sum, other_sum, own_ref, other_ref):
    other_ref[...] = (other_sum[...] + dot(far[...], out_b[2], NT)).astype(BF16)
    own_ref[...] = own_sum[...] + dot(far[...], out_a[2], NT)


def masked(pair, odd):
    lane = iota(pair.shape, 1)
    keep = lane >= 64 if odd else lane < 64
    return jnp.where(keep, pair, jnp.zeros_like(pair))


def mix_kernel(
    input_sum,
    input_other,
    to_end,
    decay_ref,
    skip_ref,
    mix_ref,
    end_ref,
    local_ref,
    weight_ref,
):
    width = local_ref.shape[1]
    mix = (input_sum[...] + input_other[...].astype(F32)).astype(BF16)
    mix_ref[...] = mix
    writer = mix[:, width : width + STATE]
    reader = mix[:, width + STATE :]
    scaled = (mix[:, :width].astype(F32) * to_end[...]).astype(BF16)
    end_ref[...] = dot(writer, scaled, TN).astype(BF16)
    scores = dot(reader, writer, NT)
    for two in range(HEADS // 2):
        at = slice(two * 128, two * 128 + 128)
        value_pair = mix[:, at]
        local = value_pair.astype(F32) * skip_ref[:, at]
        for odd in range(2):
            h = 2 * two + odd
            weight = (scores * decay_ref[h].astype(F32)).astype(BF16)
            weight_ref[h] = weight
            local = local + dot(weight, masked(value_pair, odd), NN)
        local_ref[:, at] = local


def state_kernel(mix_ref, grad_sum, grad_other, entering, end_ref, totals, grad_ref, pay_ref):
    width = grad_sum.shape[1]
    grad = (grad_sum[...] + grad_other[...].astype(F32)).astype(BF16)
    grad_ref[...] = grad
    scaled = (grad.astype(F32) * entering[...]).astype(BF16)
    reader = mix_ref[:, width + STATE :]
    pay_ref[:STATE, :width] = end_ref[...]
    pay_ref[STATE:, :width] = dot(reader, scaled, TN).astype(BF16)
    total = totals[0:1, :].astype(F32)
    pay_ref[:, width:] = jnp.broadcast_to(total, (2 * STATE, 128)).astype(BF16)


def owner_kernel(pieces_ref, out_ref, decay_ref):
    count, width = out_ref.shape[0], out_ref.shape[2]
    lanes = (128, width)
    head = iota(lanes, 1) // 64
    place = iota(lanes, 0)
    keep = (place % HEADS == head) & (place < 3 * HEADS)
    totals = pieces_ref[:, 0, width:]
    decay_ref[...] = jnp.exp(dot(totals, ones_where(keep), NN))
    back = lax.axis_index("x") >= 2
    state = jnp.zeros(out_ref.shape[1:], F32)
    for k in range(count):
        at = jnp.where(back, count - 1 - k, k)
        out_ref[at] = state.astype(BF16)
        state = state * decay_ref[pl.ds(at, 1), :] + pieces_ref[at, :, :width].astype(F32)


def output_kernel(mix_ref, states_ref, entering, local_ref, out_ref):
    width = local_ref.shape[1]
    reader = mix_ref[:, width + STATE :]
    mixed = local_ref[...] + dot(reader, states_ref[:STATE, :], NN) * entering[...]
    out_ref[...] = mixed.astype(BF16)


def gradient_kernel(
    mix_ref, grad_ref, states_ref, entering, to_end, skip_ref, weight_ref, decay_ref, out_ref
):
    rows, width = grad_ref.shape
    writer = mix_ref[:, width : width + STATE]
    reader = mix_ref[:, width + STATE :]
    incoming = states_ref[:STATE, :]
    outgoing = states_ref[STATE:, :]
    half = rows // 2
    upper = jnp.zeros((half, half), F32)
    lower = jnp.zeros((half, rows), F32)
    for two in range(HEADS // 2):
        at = slice(two * 128, two * 128 + 128)
        value_pair = mix_ref[:, at]
        grad_pair = grad_ref[:, at]
        back = grad_pair.astype(F32) * skip_ref[:, at]
        back = back + dot(writer, outgoing[:, at], NN) * to_end[:, at]
        early, late = back[:half], back[half:]
        for odd in range(2):
            h = 2 * two + odd
            grad_one = masked(grad_pair, odd)
            early = early + dot(weight_ref[h, :, :half], grad_one, TN)
            late = late + dot(weight_ref[h, half:, half:], grad_one[half:], TN)
            kernel = decay_ref[h, :half, :half].astype(F32)
            upper = upper + dot(grad_one[:half], value_pair[:half], NT) * kernel
            kernel = decay_ref[h, half:, :].astype(F32)
            lower = lower + dot(grad_one[half:], value_pair, NT) * kernel
        out_ref[:half, at] = early.astype(BF16)
        out_ref[half:, at] = late.astype(BF16)
    upper = jnp.concatenate([upper, jnp.zeros((half, half), F32)], axis=1)
    score_grad = jnp.concatenate([upper, lower], axis=0).astype(BF16)
    value_scaled = (mix_ref[:, :width].astype(F32) * to_end[...]).astype(BF16)
    write = dot(score_grad, reader, TN) + dot(value_scaled, outgoing, NT)
    out_ref[:, width : width + STATE] = write.astype(BF16)
    grad_scaled = (grad_ref[...].astype(F32) * entering[...]).astype(BF16)
    read = dot(score_grad, writer, NN) + dot(grad_scaled, incoming, NT)
    out_ref[:, width + STATE :] = read.astype(BF16)


def resolved(block):
    c = lax.axis_index("c")
    return {"A": 3 - 2 * c, "B": 1 + 2 * c}.get(block, block)


def output_blocks(blocks, fin, other, weight_a, weight_b, *outs):
    for out, block in zip(outs, blocks):
        k = resolved(block)
        total = dot(fin[...], weight_a[k], NN) + dot(other[...], weight_b[k], NN)
        out[...] = total.astype(out.dtype)


def input_blocks(blocks, fin, other, value_a, state_a, value_b, state_b, *outs):
    width = value_a.shape[2]
    for out, block in zip(outs, blocks):
        k = resolved(block)
        total = (
            dot(fin[:, :width], value_a[k], NT)
            + dot(fin[:, width:], state_a[k], NT)
            + dot(other[:, :width], value_b[k], NT)
            + dot(other[:, width:], state_b[k], NT)
        )
        out[...] = total.astype(out.dtype)


def add_kernel(groups, *refs):
    outs = refs[-groups:]
    count = (len(refs) - groups) // groups
    for g, out in enumerate(outs):
        total = refs[g * count][...].astype(F32)
        for ref in refs[g * count + 1 : (g + 1) * count]:
            total = total + ref[...].astype(F32)
        out[...] = total.astype(out.dtype)


def per_device(
    layer_input, value_weight, state_weight, output_weight, log_decay, skip_gain, output_grad
):
    rows, shard = layer_input.shape
    width, pair = value_weight.shape[1], state_weight.shape[1]
    wide = spec((rows, width))
    both = spec((rows, width + pair))
    block = spec((rows, shard))
    block_low = spec((rows, shard), BF16)

    input_low = shift(layer_input, "y", 1)
    input_high = shift(layer_input, "y", -1)
    grad_high = shift(output_grad, "y", -1)
    input_far = shift(input_low, "y", 1)
    grad_low = shift(output_grad, "y", 1)
    grad_far = shift(grad_high, "y", -1)

    sent = weights_of(True, value_weight, state_weight, output_weight, shard)
    value_b, state_b, out_b = [shift(w, "c", 1) for w in sent]
    value_a, state_a, out_a = weights_of(False, value_weight, state_weight, output_weight, shard)

    square = spec((HEADS, rows, rows), BF16)
    decays, entering, to_end, totals, skip = call(
        prepare_kernel,
        [square, wide, wide, spec((8, 128), BF16), spec((1, width))],
        log_decay,
        skip_gain.reshape(1, HEADS),
    )

    input_weights = (value_a, state_a, value_b, state_b)
    sums = call(
        input_first, [both, both], layer_input, input_low, input_high, *input_weights, flops=2**30
    )
    input_sum, input_send = call(
        input_last, [both, spec(both.shape, BF16)], input_far, *input_weights, *sums, flops=2**29
    )
    input_other = shift(input_send, "c", 1)
    mix, end, local, weights = call(
        mix_kernel,
        [spec((rows, width + pair), BF16), spec((STATE, width), BF16), wide, square],
        input_sum,
        input_other,
        to_end,
        decays,
        skip,
        flops=2**28,
    )
    sums = call(
        grad_first, [wide, wide], output_grad, grad_low, grad_high, out_a, out_b, flops=2**30
    )
    grad_sum, grad_send = call(
        grad_last, [wide, spec(wide.shape, BF16)], grad_far, out_a, out_b, *sums, flops=2**29
    )
    grad_other = shift(grad_send, "c", 1)
    grad, pay = call(
        state_kernel,
        [spec((rows, width), BF16), spec((2 * STATE, width + 128), BF16)],
        mix,
        grad_sum,
        grad_other,
        entering,
        end,
        totals,
    )
    pay, local = lax.optimization_barrier((pay, local))
    arrived = lax.all_to_all(pay.reshape(32, 8, width + 128), SEQ, 0, 0, tiled=True)
    owned = call(
        owner_kernel, [spec((32, 8, width), BF16)], arrived, scratch=[pltpu.VMEM((32, width), F32)]
    )[0]
    states = lax.all_to_all(owned, SEQ, 0, 0, tiled=True).reshape(2 * STATE, width)

    mixed = call(
        output_kernel, [spec((rows, width), BF16)], mix, states, entering, local, flops=2**25
    )[0]
    mixed_other = shift(mixed, "c", 1)
    grads = call(
        gradient_kernel,
        [spec((rows, width + pair), BF16)],
        mix,
        grad,
        states,
        entering,
        to_end,
        skip,
        weights,
        decays,
        flops=2**28,
    )[0]
    grads_other = shift(grads, "c", 1)

    def outputs(blocks, kinds):
        return call(
            functools.partial(output_blocks, blocks),
            kinds,
            mixed,
            mixed_other,
            out_a,
            out_b,
            flops=2**28 * len(blocks),
        )

    def inputs(blocks, kinds):
        return call(
            functools.partial(input_blocks, blocks),
            kinds,
            grads,
            grads_other,
            *input_weights,
            flops=2**28 * len(blocks),
        )

    add = functools.partial(add_kernel, 1)
    (out_2,) = outputs((2,), [block_low])
    out_from = ring(out_2, 1)
    (in_2,) = inputs((2,), [block_low])
    in_from = ring(in_2, 1)
    (out_a_block,) = outputs(("A",), [block_low])
    out_near = ring(out_a_block, -1)
    (in_a_block,) = inputs(("A",), [block_low])
    in_near = ring(in_a_block, -1)
    out_b_block, out_0 = outputs(("B", 0), [block] * 2)
    in_b_block, in_0 = inputs(("B", 0), [block] * 2)
    out_b_block = call(add, [block_low], out_b_block, out_from)[0]
    out_last = ring(out_b_block, 1)
    in_b_block = call(add, [block_low], in_b_block, in_from)[0]
    in_last = ring(in_b_block, 1)
    layer_output = call(add, [block_low], out_0, out_near, out_last)[0]
    input_grad = call(add, [block_low], in_0, in_near, in_last)[0]
    return (layer_output, input_grad)


def solution(mesh):
    split = Mesh(mesh.devices.reshape(4, 8, 4, 2), ("x", "z", "y", "c"))
    head = ("y", "c")
    in_specs = (
        P(SEQ, head),
        P(None, head),
        P(None, head),
        P(head, None),
        P(head, SEQ),
        P(head),
        P(SEQ, head),
    )
    return jax.shard_map(
        per_device,
        mesh=split,
        in_specs=in_specs,
        out_specs=(P(SEQ, head), P(SEQ, head)),
        check_vma=False,
    )
```
